32 devices in a mesh: dp: 8 (over y, x, core), code: 4 (over z).
Axes of the slice: x: 2, y: 2, z: 4, core: 2. Of those that a mesh axis runs over, the one named last changes fastest.
Arguments:
- temporal_out: bfloat16 [1024, 4096], P('dp'), may hold values from -6 to 6
- depth_in: bfloat16 [4, 4096, 1024], P('code', 'dp'), may hold values from -0.09375 to 0.09375
- embed: bfloat16 [4, 1024, 1024], P('code'), may hold values from -6 to 6
- depth_w1: bfloat16 [4, 1024, 2112], P('code', None, 'dp'), may hold values from -0.1875 to 0.1875
- depth_w2: bfloat16 [4, 1024, 2112], P('code', None, 'dp'), may hold values from -0.125 to 0.125
- audio_tokens: int32 [1024, 4], P(None, 'code'), may hold values from 0 to 1023
- barge_mask: int32 [1024], P('dp'), may hold values 0 or 1
- out_grad: bfloat16 [1024, 4, 1024], P('dp', 'code'), may hold values from -6 to 6
Outputs:
- temporal_grad: bfloat16 [1024, 4096], P('dp', 'code')
- depth_in_grad: bfloat16 [4, 4096, 1024], P('code', 'dp')
- embed_grad: bfloat16 [4, 1024, 1024], P('code', 'dp')
- w1_grad: bfloat16 [4, 1024, 2112], P('code', None, 'dp')
- w2_grad: bfloat16 [4, 1024, 2112], P('code', None, 'dp')
The draws below stay inside these ranges and needn't reach their ends.
All inputs are finite; a program needn't handle non-finite values. No bound on the sum of `barge_mask` on one device may be relied on, other than what follows from the above.
Results may differ from the reference program's by a relative error of at most 0.02.
Values may be sent and summed in bfloat16 or wider, within the bound.
A program may use at most 128 MiB of HBM per device.

```python
import jax
import jax.numpy as jnp
from jax import lax

D = 4096
DD = 1024
DH = 2112
V = 1024
ROWS_DEV = 128
FRAMES = 1024
CODEBOOKS = 4
N_DP = 8


def plant(entries, key, least, high):
    place = [jax.random.randint(jax.random.fold_in(key, axis), (), 0, length) for axis, length in enumerate(entries.shape)]
    main_axis = entries.shape.index(max(entries.shape))
    next_to = place[:main_axis] + [(place[main_axis] + 1) % entries.shape[main_axis]] + place[main_axis + 1:]
    return entries.at[tuple(place)].set(least).at[tuple(next_to)].set(high)


def levels(key, shape, cuts, low, top_value):
    def one(position, parts):
        heights = jax.random.uniform(jax.random.fold_in(jax.random.fold_in(key, 6), position), (parts,), jnp.float32, low / len(cuts), top_value / len(cuts))
        return jnp.repeat(jnp.exp(heights), shape[position] // parts).reshape((-1,) + (1,) * (len(shape) - position - 1))

    gain = one(*cuts[0])
    for cut in cuts[1:]:
        gain = gain * one(*cut)
    return gain


def noise(key, extent, deviation, bound, pieces=(), held_as=jnp.bfloat16):
    level = levels(key, extent, pieces, -0.22, 0.18) if pieces else 1.0
    values = jax.random.normal(key, extent, jnp.float32) * deviation * level
    return jnp.minimum(jnp.maximum(values, -bound), bound).astype(held_as)


def setup_inputs(seed: int = 0) -> dict:
    streams_of = jax.random.split(jax.random.key(seed), 9)
    return {
        "temporal_out": noise(streams_of[0], (FRAMES, D), 1.0, 6.0, ((0, 8),)),
        "depth_in": noise(streams_of[1], (CODEBOOKS, D, DD), D ** -0.5, 0.09375, ((0, 4), (1, 8))),
        "embed": noise(streams_of[2], (CODEBOOKS, V, DD), 1.0, 6.0, ((0, 4),)),
        "depth_w1": noise(streams_of[3], (CODEBOOKS, DD, DH), DD ** -0.5, 0.1875, ((0, 4), (2, 8))),
        "depth_w2": noise(streams_of[4], (CODEBOOKS, DD, DH), DH ** -0.5, 0.125, ((0, 4), (2, 8))),
        "audio_tokens": plant(jax.random.randint(streams_of[5], (FRAMES, CODEBOOKS), 0, V), jax.random.fold_in(streams_of[5], 1), 0, V - 1).astype(jnp.int32),
        "barge_mask": plant((jax.random.randint(streams_of[6], (FRAMES,), 0, 2) < 1).astype(jnp.int32), jax.random.fold_in(streams_of[6], 1), 0, 1),
        "out_grad": noise(streams_of[7], (FRAMES, CODEBOOKS, DD), 1.0, 6.0, ((0, 8), (1, 4))),
    }


EPS = 1e-06

def matmul(left, right):
    return jnp.dot(left, right, preferred_element_type=jnp.float32)

def contract_rows(left, right):
    return lax.dot_general(left, right, (((0,), (0,)), ((), ())), preferred_element_type=jnp.float32)

def contract_cols(left, right):
    return lax.dot_general(left, right, (((1,), (1,)), ((), ())), preferred_element_type=jnp.float32)

def silu_slope(values):
    sigma = jax.nn.sigmoid(values)
    return sigma * (1.0 + values * (1.0 - sigma))

def group_sum(left, right):
    total = jnp.zeros((left.shape[1], right.shape[1]), jnp.float32)
    for group in range(N_DP):
        first = group * ROWS_DEV
        part = contract_rows(left[first:first + ROWS_DEV], right[first:first + ROWS_DEV]).astype(jnp.bfloat16)
        total = total + part.astype(jnp.float32)
    return total.astype(jnp.bfloat16)

def reference(temporal_out, depth_in, embed, depth_w1, depth_w2, audio_tokens, barge_mask, out_grad):
    row_weight = barge_mask.astype(jnp.float32)[:, None]
    incoming = jnp.zeros((FRAMES, DD), jnp.bfloat16)
    saved = []
    for book in range(CODEBOOKS):
        table_rows = jnp.take(embed[book], audio_tokens[:, book], axis=0).astype(jnp.float32)
        resid = matmul(temporal_out, depth_in[book]) + table_rows + incoming.astype(jnp.float32)
        scale = lax.rsqrt(lax.optimization_barrier(jnp.mean(resid * resid, axis=-1, keepdims=True)) + EPS)
        normed = (resid * scale).astype(jnp.bfloat16)
        pre_act = matmul(normed, depth_w1[book])
        active = jax.nn.silu(pre_act).astype(jnp.bfloat16)
        incoming = (resid + contract_cols(active, depth_w2[book])).astype(jnp.bfloat16)
        saved.append((resid, scale, normed, pre_act, active))
    vocab_ids = jnp.arange(V, dtype=jnp.int32)[None, :]
    from_next = jnp.zeros((FRAMES, DD), jnp.bfloat16)
    temporal_slope = jnp.zeros((FRAMES, D), jnp.float32)
    w1_list = [None] * CODEBOOKS
    w2_list = [None] * CODEBOOKS
    in_list = [None] * CODEBOOKS
    embed_list = [None] * CODEBOOKS
    for book in reversed(range(CODEBOOKS)):
        resid, scale, normed, pre_act, active = saved[book]
        state_slope = out_grad[:, book, :].astype(jnp.float32) * row_weight + from_next.astype(jnp.float32)
        slope_b = state_slope.astype(jnp.bfloat16)
        pre_slope = (matmul(slope_b, depth_w2[book]) * silu_slope(pre_act)).astype(jnp.bfloat16)
        norm_slope = contract_cols(pre_slope, depth_w1[book])
        unit_rows = resid * scale
        from_next = (state_slope + scale * (norm_slope - unit_rows * lax.optimization_barrier(jnp.mean(norm_slope * unit_rows, axis=-1, keepdims=True)))).astype(jnp.bfloat16)
        w1_list[book] = group_sum(normed, pre_slope)
        w2_list[book] = group_sum(slope_b, active)
        in_list[book] = group_sum(temporal_out, from_next)
        onehot = (audio_tokens[:, book][:, None] == vocab_ids).astype(jnp.bfloat16)
        embed_list[book] = group_sum(onehot, from_next)
        term = contract_cols(from_next, depth_in[book]).astype(jnp.bfloat16)
        temporal_slope = temporal_slope + term.astype(jnp.float32)
    temporal_grad = temporal_slope.astype(jnp.bfloat16)
    return (temporal_grad, jnp.stack(in_list), jnp.stack(embed_list), jnp.stack(w1_list), jnp.stack(w2_list))
```

```python
import functools

import jax
import jax.numpy as jnp
from jax import lax
from jax.experimental import pallas as pl
from jax.experimental.pallas import tpu as pltpu
from jax.sharding import PartitionSpec as P

EPS = 1e-06
MESH = pl.DeviceIdType.MESH
CHUNKS = 2
TILE = 512


def dot_nt(left, right):
    return lax.dot_general(
        left, right, (((1,), (1,)), ((), ())), preferred_element_type=jnp.float32
    )


def dot_nn(left, right):
    return jnp.dot(left, right, preferred_element_type=jnp.float32)


def chain_kernel(
    n_dp,
    n_code,
    temporal,
    embedded,
    cot_ref,
    proj_own,
    w1_own,
    w2_own,
    temporal_grad,
    cols_all,
    normed_all,
    slope_all,
    carry_all,
    act_all,
    pre_all,
    proj,
    w1,
    w2,
    base,
    acc,
    incoming,
    returning,
    state,
    carry_out,
    deriv,
    act_t,
    pre_t,
    scale_ref,
    term,
    term_in,
    ring_send,
    ring_recv,
    pass_send,
    pass_recv,
    own_sem,
    chain_send,
    chain_recv,
    ag_send,
    ag_recv,
    swap_send,
    swap_recv,
    term_send,
    term_recv,
):
    dp = lax.axis_index("dp")
    code = lax.axis_index("code")
    rows, width = base.shape
    hidden = w1.shape[0]
    pad = hidden // n_dp
    depth = proj_own.shape[0]
    half = width // 2
    step_rows = rows // CHUNKS
    chips = n_dp // 2
    core = lax.rem(dp, 2)
    chip = dp // 2
    partner = chip * 2 + 1 - core

    def ring_place(c):
        return jnp.where(lax.rem(c, 2) == 0, c // 2, chips - 1 - c // 2)

    def ring_chip(p):
        p = lax.rem(p + 2 * chips, chips)
        return jnp.where(p < chips // 2, 2 * p, 2 * (chips - 1 - p) + 1)

    place = ring_place(chip)
    right = ring_chip(place + 1) * 2 + core
    left = ring_chip(place - 1) * 2 + core

    barrier = pltpu.get_barrier_semaphore()
    for other in range(1, n_dp):
        pl.semaphore_signal(
            barrier, inc=1, device_id=(lax.rem(dp + other, n_dp), code), device_id_type=MESH
        )
    for other in range(1, n_code):
        pl.semaphore_signal(
            barrier, inc=1, device_id=(dp, lax.rem(code + other, n_code)), device_id_type=MESH
        )
    pl.semaphore_wait(barrier, n_dp + n_code - 2)

    whole = (
        (proj_own, proj, depth),
        (w1_own, w1, pad),
        (w2_own, w2, pad),
    )

    def part(array, size, owner, way):
        start = pl.multiple_of(owner * size, 16)
        return array.at[pl.ds(start, size), pl.ds(way * half, half)]

    def ring_copy(i, way, step):
        own, full, size = whole[i]
        origin = ring_chip(place - step if way == 0 else place + step) * 2 + core
        dst = part(full, size, origin, way)
        src = own.at[:, pl.ds(way * half, half)] if step == 0 else dst
        return pltpu.make_async_remote_copy(
            src_ref=src,
            dst_ref=dst,
            send_sem=ring_send.at[i, way, step],
            recv_sem=ring_recv.at[i, way, step],
            device_id=(right if way == 0 else left, code),
            device_id_type=MESH,
        )

    def pass_copy(i, way, step):
        own, full, size = whole[i]
        origin = ring_chip(place - step if way == 0 else place + step) * 2 + core
        dst = part(full, size, origin, way)
        src = own.at[:, pl.ds(way * half, half)] if step == 0 else dst
        return pltpu.make_async_remote_copy(
            src_ref=src,
            dst_ref=dst,
            send_sem=pass_send.at[i, way, step],
            recv_sem=pass_recv.at[i, way, step],
            device_id=(partner, code),
            device_id_type=MESH,
        )

    def own_copy(i):
        own, full, size = whole[i]
        start = pl.multiple_of(dp * size, 16)
        return pltpu.make_async_copy(own, full.at[pl.ds(start, size), :], own_sem.at[i])

    def add_base(origin, way):
        lanes = pl.ds(way * half, half)
        base[:, lanes] += dot_nn(
            temporal[:, pl.ds(pl.multiple_of(origin * depth, 128), depth)],
            proj[pl.ds(pl.multiple_of(origin * depth, 16), depth), lanes],
        )

    for i in range(3):
        for way in range(2):
            ring_copy(i, way, 0).start()
    for i in range(3):
        for way in range(2):
            pass_copy(i, way, 0).start()
        own_copy(i).start()
    base[...] = embedded[...].astype(jnp.float32)
    own_copy(0).wait()
    for way in range(2):
        add_base(dp, way)
    for step in range(1, chips):
        for i in range(3):
            for way in range(2):
                ring_copy(i, way, step - 1).wait_recv()
                if step < chips - 1:
                    ring_copy(i, way, step).start()
                pass_copy(i, way, step).start()
            if i == 0:
                for way in range(2):
                    add_base(ring_chip(place - step if way == 0 else place + step) * 2 + core, way)
                for way in range(2):
                    pass_copy(0, way, step - 1).wait_recv()
                    add_base(
                        ring_chip(place - step + 1 if way == 0 else place + step - 1) * 2 + 1 - core,
                        way,
                    )
    for way in range(2):
        pass_copy(0, way, chips - 1).wait_recv()
        add_base(
            ring_chip(place - chips + 1 if way == 0 else place + chips - 1) * 2 + 1 - core, way
        )

    def swap_copy(i, other):
        target = lax.rem(dp + other, n_dp)
        if i == 0:
            src = temporal.at[:, pl.ds(pl.multiple_of(target * depth, 128), depth)]
            dst = cols_all.at[dp]
        else:
            table, full = ((act_t, act_all), (pre_t, pre_all))[i - 1]
            src = table.at[pl.ds(pl.multiple_of(target * pad, 16), pad), :]
            dst = full.at[dp]
        return pltpu.make_async_remote_copy(
            src_ref=src,
            dst_ref=dst,
            send_sem=swap_send.at[i, other],
            recv_sem=swap_recv.at[i, other],
            device_id=(target, code),
            device_id_type=MESH,
        )

    gathered = (normed_all, slope_all, carry_all)

    def peer_copy(i, other):
        block = gathered[i].at[dp]
        target = lax.rem(dp + 2 * other, n_dp)
        return pltpu.make_async_remote_copy(
            src_ref=block,
            dst_ref=block,
            send_sem=ag_send.at[i, 0, other],
            recv_sem=ag_recv.at[i, 0, other],
            device_id=(target, code),
            device_id_type=MESH,
        )

    def hand_copy(i, other):
        block = gathered[i].at[lax.rem(dp - 2 * other + n_dp, n_dp)]
        return pltpu.make_async_remote_copy(
            src_ref=block,
            dst_ref=block,
            send_sem=ag_send.at[i, 1, other],
            recv_sem=ag_recv.at[i, 1, other],
            device_id=(partner, code),
            device_id_type=MESH,
        )

    def gather_start(i):
        for other in range(1, chips):
            peer_copy(i, other).start()
        hand_copy(i, 0).start()

    def gather_forward(i):
        for other in range(1, chips):
            peer_copy(i, other).wait_recv()
            hand_copy(i, other).start()

    def gather_finish(i):
        for other in range(1, chips):
            peer_copy(i, other).wait_send()
        for other in range(chips):
            hand_copy(i, other).wait()

    def chain_copy(way, c):
        chunk = pl.ds(c * step_rows, step_rows)
        src, dst = ((state, incoming), (carry_out, returning))[way]
        target = lax.rem(code + (1 if way == 0 else n_code - 1), n_code)
        return pltpu.make_async_remote_copy(
            src_ref=src.at[chunk, :],
            dst_ref=dst.at[chunk, :],
            send_sem=chain_send.at[way, c],
            recv_sem=chain_recv.at[way, c],
            device_id=(dp, target),
            device_id_type=MESH,
        )

    first = code == 0
    last = code == n_code - 1

    @pl.when(first)
    def _():
        incoming[...] = jnp.zeros_like(incoming)

    @pl.when(last)
    def _():
        returning[...] = jnp.zeros_like(returning)

    for i in range(1, 3):
        own_copy(i).wait()
        for way in range(2):
            for step in range(chips):
                pass_copy(i, way, step).wait_recv()
    for other in range(1, n_dp):
        swap_copy(0, other).start()
    cols_all[dp] = temporal[:, pl.ds(pl.multiple_of(dp * depth, 128), depth)]

    tiles = hidden // TILE
    rest = hidden - tiles * TILE

    def over_tiles(body):
        def turn(t, carry):
            body(pl.multiple_of(t * TILE, TILE), TILE)
            return carry

        lax.fori_loop(0, tiles, turn, 0)
        if rest:
            body(tiles * TILE, rest)

    for c in range(CHUNKS):
        chunk = pl.ds(c * step_rows, step_rows)

        @pl.when(jnp.logical_not(first))
        def _():
            chain_copy(0, c).wait_recv()

        resid = base[chunk, :] + incoming[chunk, :].astype(jnp.float32)
        base[chunk, :] = resid
        scale = lax.rsqrt(jnp.mean(resid * resid, axis=-1, keepdims=True) + EPS)
        scale_ref[chunk, :] = jnp.broadcast_to(scale, (step_rows, 128))
        normed_all[dp, chunk, :] = (resid * scale).astype(jnp.bfloat16)
        acc[chunk, :] = resid

        def forward(start, size):
            lanes = pl.ds(start, size)
            pre = dot_nt(normed_all[dp, chunk, :], w1[lanes, :])
            deriv[chunk, lanes] = pre
            active = (pre * jax.nn.sigmoid(pre)).astype(jnp.bfloat16)
            acc[chunk, :] += dot_nn(active, w2[lanes, :])

        over_tiles(forward)
        state[chunk, :] = acc[chunk, :].astype(jnp.bfloat16)

        @pl.when(jnp.logical_not(last))
        def _():
            chain_copy(0, c).start()

    gather_start(0)

    def slopes(start, size):
        lanes = pl.ds(start, size)
        pre = deriv[:, lanes]
        sigma = jax.nn.sigmoid(pre)
        active = pre * sigma
        deriv[:, lanes] = sigma * (1.0 + pre * (1.0 - sigma))
        act_t[lanes, :] = active.T.astype(jnp.bfloat16)

    over_tiles(slopes)
    for other in range(1, n_dp):
        swap_copy(1, other).start()
    act_all[dp] = act_t[pl.ds(pl.multiple_of(dp * pad, 16), pad), :]
    gather_forward(0)

    for c in range(CHUNKS):
        chunk = pl.ds(c * step_rows, step_rows)

        @pl.when(jnp.logical_not(last))
        def _():
            chain_copy(1, c).wait_recv()

        slope = cot_ref[chunk, :].astype(jnp.float32) + returning[chunk, :].astype(jnp.float32)
        slope_all[dp, chunk, :] = slope.astype(jnp.bfloat16)
        acc[chunk, :] = jnp.zeros((step_rows, width), jnp.float32)

        def backward(start, size):
            lanes = pl.ds(start, size)
            back = dot_nt(slope_all[dp, chunk, :], w2[lanes, :])
            pre_slope = back * deriv[chunk, lanes]
            deriv[chunk, lanes] = pre_slope
            acc[chunk, :] += dot_nn(pre_slope.astype(jnp.bfloat16), w1[lanes, :])

        over_tiles(backward)
        norm_slope = acc[chunk, :]
        scale = scale_ref[chunk, 0:1]
        unit = base[chunk, :] * scale
        slope = cot_ref[chunk, :].astype(jnp.float32) + returning[chunk, :].astype(jnp.float32)
        carried = (
            slope
            + scale * (norm_slope - unit * jnp.mean(norm_slope * unit, axis=-1, keepdims=True))
        ).astype(jnp.bfloat16)
        carry_out[chunk, :] = carried
        carry_all[dp, chunk, :] = carried

        @pl.when(jnp.logical_not(first))
        def _():
            chain_copy(1, c).start()

    gather_start(2)
    gather_start(1)

    quarter = term.shape[2]
    per = quarter // depth

    def terms(j, carry):
        rows_j = pl.ds(pl.multiple_of(j * depth, 16), depth)
        value = dot_nt(carry_all[dp], proj[rows_j, :]).astype(jnp.bfloat16)
        term[j // per, :, pl.ds(pl.multiple_of(lax.rem(j, per) * depth, 128), depth)] = value
        return carry

    lax.fori_loop(0, n_dp, terms, 0)

    def term_copy(other):
        target = lax.rem(code + other, n_code)
        return pltpu.make_async_remote_copy(
            src_ref=term.at[target],
            dst_ref=term_in.at[other],
            send_sem=term_send.at[other],
            recv_sem=term_recv.at[other],
            device_id=(dp, target),
            device_id_type=MESH,
        )

    for other in range(1, n_code):
        term_copy(other).start()

    def turn_over(start, size):
        lanes = pl.ds(start, size)
        pre_t[lanes, :] = deriv[:, lanes].T.astype(jnp.bfloat16)

    over_tiles(turn_over)
    for other in range(1, n_dp):
        swap_copy(2, other).start()
    pre_all[dp] = pre_t[pl.ds(pl.multiple_of(dp * pad, 16), pad), :]

    gather_forward(2)
    gather_forward(1)
    total = term[code].astype(jnp.float32)
    for other in range(1, n_code):
        term_copy(other).wait_recv()
        total += term_in[other].astype(jnp.float32)
    temporal_grad[...] = total.astype(jnp.bfloat16)

    for i in range(3):
        for way in range(2):
            for step in range(chips - 1):
                ring_copy(i, way, step).wait_send()
            for step in range(chips):
                pass_copy(i, way, step).wait_send()
    for c in range(CHUNKS):

        @pl.when(jnp.logical_not(last))
        def _():
            chain_copy(0, c).wait_send()

        @pl.when(jnp.logical_not(first))
        def _():
            chain_copy(1, c).wait_send()

    for i in range(3):
        gather_finish(i)
        for other in range(1, n_dp):
            swap_copy(i, other).wait()
    for other in range(1, n_code):
        term_copy(other).wait_send()


def per_device(
    temporal_out, depth_in, embed, depth_w1, depth_w2, audio_tokens, barge_mask, out_grad
):
    dp_index = lax.axis_index("dp")
    n_code = lax.axis_size("code")
    n_dp = lax.axis_size("dp")
    rows, wide = temporal_out.shape
    depth, width = depth_in.shape[1:]
    share = depth_w1.shape[2]
    pad = -(-share // 16) * 16
    hidden = pad * n_dp
    quarter = wide // n_code
    chips = n_dp // 2
    table = embed[0]
    token_all = audio_tokens[:, 0]
    token_own = lax.dynamic_slice_in_dim(token_all, dp_index * rows, rows, 0)
    embedded = jnp.take(table, token_own, axis=0)
    cotangent = out_grad[:, 0, :] * barge_mask.astype(jnp.bfloat16)[:, None]
    w1_own = jnp.pad(depth_w1[0].T, ((0, pad - share), (0, 0)))
    w2_own = jnp.pad(depth_w2[0].T, ((0, pad - share), (0, 0)))

    bf16, f32 = jnp.bfloat16, jnp.float32
    vmem = pl.BlockSpec(memory_space=pltpu.VMEM)
    hbm = pl.BlockSpec(memory_space=pl.ANY)
    dma = pltpu.SemaphoreType.DMA
    out_shape = (
        jax.ShapeDtypeStruct((rows, quarter), bf16),
        jax.ShapeDtypeStruct((n_dp, rows, depth), bf16),
        jax.ShapeDtypeStruct((n_dp, rows, width), bf16),
        jax.ShapeDtypeStruct((n_dp, rows, width), bf16),
        jax.ShapeDtypeStruct((n_dp, rows, width), bf16),
        jax.ShapeDtypeStruct((n_dp, pad, rows), bf16),
        jax.ShapeDtypeStruct((n_dp, pad, rows), bf16),
    )
    temporal_grad, cols_all, normed_all, slope_all, carry_all, act_all, pre_all = pl.pallas_call(
        functools.partial(chain_kernel, n_dp, n_code),
        out_shape=out_shape,
        in_specs=[vmem, vmem, vmem, hbm, hbm, hbm],
        out_specs=(vmem,) * 7,
        scratch_shapes=[
            pltpu.VMEM((wide, width), bf16),
            pltpu.VMEM((hidden, width), bf16),
            pltpu.VMEM((hidden, width), bf16),
            pltpu.VMEM((rows, width), f32),
            pltpu.VMEM((rows, width), f32),
            pltpu.VMEM((rows, width), bf16),
            pltpu.VMEM((rows, width), bf16),
            pltpu.VMEM((rows, width), bf16),
            pltpu.VMEM((rows, width), bf16),
            pltpu.VMEM((rows, hidden), f32),
            pltpu.VMEM((hidden, rows), bf16),
            pltpu.VMEM((hidden, rows), bf16),
            pltpu.VMEM((rows, 128), f32),
            pltpu.VMEM((n_code, rows, quarter), bf16),
            pltpu.VMEM((n_code, rows, quarter), bf16),
            dma((3, 2, chips)),
            dma((3, 2, chips)),
            dma((3, 2, chips)),
            dma((3, 2, chips)),
            dma((3,)),
            dma((2, CHUNKS)),
            dma((2, CHUNKS)),
            dma((3, 2, chips)),
            dma((3, 2, chips)),
            dma((3, n_dp)),
            dma((3, n_dp)),
            dma((n_code,)),
            dma((n_code,)),
        ],
        compiler_params=pltpu.CompilerParams(
            collective_id=0, has_side_effects=True, vmem_limit_bytes=60 * 1024 * 1024
        ),
        name="depth_chain",
    )(temporal_out, embedded, cotangent, depth_in[0], w1_own, w2_own)

    def over_rows(left, right):
        return lax.dot_general(
            left, right, (((0,), (0,)), ((), ())), preferred_element_type=jnp.float32
        )

    frames = n_dp * rows
    normed = normed_all.reshape(frames, width)
    slope = slope_all.reshape(frames, width)
    carry = carry_all.reshape(frames, width)
    columns = cols_all.reshape(frames, depth)
    pre_rows = pre_all[:, :share, :].transpose(0, 2, 1).reshape(frames, share)
    act_rows = act_all[:, :share, :].transpose(0, 2, 1).reshape(frames, share)
    first_grad = over_rows(normed, pre_rows).astype(bf16)
    second_grad = over_rows(slope, act_rows).astype(bf16)
    proj_grad = over_rows(columns, carry).astype(bf16)
    vocab_local = table.shape[0] // n_dp
    vocab_ids = lax.broadcasted_iota(jnp.int32, (1, vocab_local), 1) + dp_index * vocab_local
    onehot = (token_all[:, None] == vocab_ids).astype(bf16)
    table_grad = over_rows(onehot, carry).astype(bf16)
    return (
        temporal_grad,
        proj_grad[None],
        table_grad[None],
        first_grad[None],
        second_grad[None],
    )


def solution(mesh):
    in_specs = (
        P("dp", None),
        P("code", "dp", None),
        P("code", None, None),
        P("code", None, "dp"),
        P("code", None, "dp"),
        P(None, "code"),
        P("dp"),
        P("dp", "code", None),
    )
    out_specs = (
        P("dp", "code"),
        P("code", "dp", None),
        P("code", "dp", None),
        P("code", None, "dp"),
        P("code", None, "dp"),
    )
    return jax.shard_map(
        per_device, mesh=mesh, in_specs=in_specs, out_specs=out_specs, check_vma=False
    )
```

```python
import functools

import jax
import jax.numpy as jnp
from jax import lax
from jax.experimental import pallas as pl
from jax.experimental.pallas import tpu as pltpu
from jax.sharding import PartitionSpec as P

EPS = 1e-06
MESH = pl.DeviceIdType.MESH
CHUNKS = 2
TILE = 512


def dot_nt(left, right):
    return lax.dot_general(
        left, right, (((1,), (1,)), ((), ())), preferred_element_type=jnp.float32
    )


def dot_nn(left, right):
    return jnp.dot(left, right, preferred_element_type=jnp.float32)


def chain_kernel(
    n_dp,
    n_code,
    temporal,
    embedded,
    cot_ref,
    proj_own,
    w1_own,
    w2_own,
    temporal_grad,
    cols_all,
    normed_all,
    slope_all,
    carry_all,
    act_all,
    pre_all,
    proj,
    w1,
    w2,
    base,
    acc,
    incoming,
    returning,
    state,
    carry_out,
    deriv,
    act_t,
    pre_t,
    scale_ref,
    term,
    term_in,
    ring_send,
    ring_recv,
    pass_send,
    pass_recv,
    own_sem,
    chain_send,
    chain_recv,
    ag_send,
    ag_recv,
    swap_send,
    swap_recv,
    term_send,
    term_recv,
):
    dp = lax.axis_index("dp")
    code = lax.axis_index("code")
    rows, width = base.shape
    hidden = w1.shape[0]
    pad = hidden // n_dp
    depth = proj_own.shape[0]
    half = width // 2
    step_rows = rows // CHUNKS
    chips = n_dp // 2
    core = lax.rem(dp, 2)
    chip = dp // 2
    partner = chip * 2 + 1 - core

    def ring_place(c):
        return jnp.where(lax.rem(c, 2) == 0, c // 2, chips - 1 - c // 2)

    def ring_chip(p):
        p = lax.rem(p + 2 * chips, chips)
        return jnp.where(p < chips // 2, 2 * p, 2 * (chips - 1 - p) + 1)

    place = ring_place(chip)
    right = ring_chip(place + 1) * 2 + core
    left = ring_chip(place - 1) * 2 + core

    barrier = pltpu.get_barrier_semaphore()
    for other in range(1, n_dp):
        pl.semaphore_signal(
            barrier, inc=1, device_id=(lax.rem(dp + other, n_dp), code), device_id_type=MESH
        )
    for other in range(1, n_code):
        pl.semaphore_signal(
            barrier, inc=1, device_id=(dp, lax.rem(code + other, n_code)), device_id_type=MESH
        )
    pl.semaphore_wait(barrier, n_dp + n_code - 2)

    whole = (
        (proj_own, proj, depth),
        (w1_own, w1, pad),
        (w2_own, w2, pad),
    )

    def part(array, size, owner, way):
        start = pl.multiple_of(owner * size, 16)
        return array.at[pl.ds(start, size), pl.ds(way * half, half)]

    def ring_copy(i, way, step):
        own, full, size = whole[i]
        origin = ring_chip(place - step if way == 0 else place + step) * 2 + core
        dst = part(full, size, origin, way)
        src = own.at[:, pl.ds(way * half, half)] if step == 0 else dst
        return pltpu.make_async_remote_copy(
            src_ref=src,
            dst_ref=dst,
            send_sem=ring_send.at[i, way, step],
            recv_sem=ring_recv.at[i, way, step],
            device_id=(right if way == 0 else left, code),
            device_id_type=MESH,
        )

    def pass_copy(i, way, step):
        own, full, size = whole[i]
        origin = ring_chip(place - step if way == 0 else place + step) * 2 + core
        dst = part(full, size, origin, way)
        src = own.at[:, pl.ds(way * half, half)] if step == 0 else dst
        return pltpu.make_async_remote_copy(
            src_ref=src,
            dst_ref=dst,
            send_sem=pass_send.at[i, way, step],
            recv_sem=pass_recv.at[i, way, step],
            device_id=(partner, code),
            device_id_type=MESH,
        )

    def own_copy(i):
        own, full, size = whole[i]
        start = pl.multiple_of(dp * size, 16)
        return pltpu.make_async_copy(own, full.at[pl.ds(start, size), :], own_sem.at[i])

    def add_base(origin, way):
        lanes = pl.ds(way * half, half)
        base[:, lanes] += dot_nn(
            temporal[:, pl.ds(pl.multiple_of(origin * depth, 128), depth)],
            proj[pl.ds(pl.multiple_of(origin * depth, 16), depth), lanes],
        )

    for i in range(3):
        for way in range(2):
            ring_copy(i, way, 0).start()
    for i in range(3):
        for way in range(2):
            pass_copy(i, way, 0).start()
        own_copy(i).start()
    base[...] = embedded[...].astype(jnp.float32)
    own_copy(0).wait()
    for way in range(2):
        add_base(dp, way)
    for step in range(1, chips):
        for i in range(3):
            for way in range(2):
                ring_copy(i, way, step - 1).wait_recv()
                if step < chips - 1:
                    ring_copy(i, way, step).start()
                pass_copy(i, way, step).start()
            if i == 0:
                for way in range(2):
                    add_base(ring_chip(place - step if way == 0 else place + step) * 2 + core, way)
                for way in range(2):
                    pass_copy(0, way, step - 1).wait_recv()
                    add_base(
                        ring_chip(place - step + 1 if way == 0 else place + step - 1) * 2 + 1 - core,
                        way,
                    )
    for way in range(2):
        pass_copy(0, way, chips - 1).wait_recv()
        add_base(
            ring_chip(place - chips + 1 if way == 0 else place + chips - 1) * 2 + 1 - core, way
        )

    def swap_copy(i, other):
        target = lax.rem(dp + other, n_dp)
        if i == 0:
            src = temporal.at[:, pl.ds(pl.multiple_of(target * depth, 128), depth)]
            dst = cols_all.at[dp]
        else:
            table, full = ((act_t, act_all), (pre_t, pre_all))[i - 1]
            src = table.at[pl.ds(pl.multiple_of(target * pad, 16), pad), :]
            dst = full.at[dp]
        return pltpu.make_async_remote_copy(
            src_ref=src,
            dst_ref=dst,
            send_sem=swap_send.at[i, other],
            recv_sem=swap_recv.at[i, other],
            device_id=(target, code),
            device_id_type=MESH,
        )

    gathered = (normed_all, slope_all, carry_all)

    def peer_copy(i, other):
        block = gathered[i].at[dp]
        target = lax.rem(dp + 2 * other, n_dp)
        return pltpu.make_async_remote_copy(
            src_ref=block,
            dst_ref=block,
            send_sem=ag_send.at[i, 0, other],
            recv_sem=ag_recv.at[i, 0, other],
            device_id=(target, code),
            device_id_type=MESH,
        )

    def hand_copy(i, other):
        block = gathered[i].at[lax.rem(dp - 2 * other + n_dp, n_dp)]
        return pltpu.make_async_remote_copy(
            src_ref=block,
            dst_ref=block,
            send_sem=ag_send.at[i, 1, other],
            recv_sem=ag_recv.at[i, 1, other],
            device_id=(partner, code),
            device_id_type=MESH,
        )

    def gather_start(i):
        for other in range(1, chips):
            peer_copy(i, other).start()
        hand_copy(i, 0).start()

    def gather_forward(i):
        for other in range(1, chips):
            peer_copy(i, other).wait_recv()
            hand_copy(i, other).start()

    def gather_finish(i):
        for other in range(1, chips):
            peer_copy(i, other).wait_send()
        for other in range(chips):
            hand_copy(i, other).wait()

    def chain_copy(way, c):
        chunk = pl.ds(c * step_rows, step_rows)
        src, dst = ((state, incoming), (carry_out, returning))[way]
        target = lax.rem(code + (1 if way == 0 else n_code - 1), n_code)
        return pltpu.make_async_remote_copy(
            src_ref=src.at[chunk, :],
            dst_ref=dst.at[chunk, :],
            send_sem=chain_send.at[way, c],
            recv_sem=chain_recv.at[way, c],
            device_id=(dp, target),
            device_id_type=MESH,
        )

    first = code == 0
    last = code == n_code - 1

    @pl.when(first)
    def _():
        incoming[...] = jnp.zeros_like(incoming)

    @pl.when(last)
    def _():
        returning[...] = jnp.zeros_like(returning)

    for i in range(1, 3):
        own_copy(i).wait()
        for way in range(2):
            for step in range(chips):
                pass_copy(i, way, step).wait_recv()
    for other in range(1, n_dp):
        swap_copy(0, other).start()
    cols_all[dp] = temporal[:, pl.ds(pl.multiple_of(dp * depth, 128), depth)]

    tiles = hidden // TILE
    rest = hidden - tiles * TILE

    def over_tiles(body):
        def turn(t, carry):
            body(pl.multiple_of(t * TILE, TILE), TILE)
            return carry

        lax.fori_loop(0, tiles, turn, 0)
        if rest:
            body(tiles * TILE, rest)

    for c in range(CHUNKS):
        chunk = pl.ds(c * step_rows, step_rows)

        @pl.when(jnp.logical_not(first))
        def _():
            chain_copy(0, c).wait_recv()

        resid = base[chunk, :] + incoming[chunk, :].astype(jnp.float32)
        base[chunk, :] = resid
        scale = lax.rsqrt(jnp.mean(resid * resid, axis=-1, keepdims=True) + EPS)
        scale_ref[chunk, :] = jnp.broadcast_to(scale, (step_rows, 128))
        normed_all[dp, chunk, :] = (resid * scale).astype(jnp.bfloat16)
        acc[chunk, :] = resid

        def forward(start, size):
            lanes = pl.ds(start, size)
            pre = dot_nt(normed_all[dp, chunk, :], w1[lanes, :])
            deriv[chunk, lanes] = pre
            active = (pre * jax.nn.sigmoid(pre)).astype(jnp.bfloat16)
            acc[chunk, :] += dot_nn(active, w2[lanes, :])

        over_tiles(forward)
        state[chunk, :] = acc[chunk, :].astype(jnp.bfloat16)

        @pl.when(jnp.logical_not(last))
        def _():
            chain_copy(0, c).start()

    gather_start(0)

    def slopes(start, size):
        lanes = pl.ds(start, size)
        pre = deriv[:, lanes]
        sigma = jax.nn.sigmoid(pre)
        active = pre * sigma
        deriv[:, lanes] = sigma * (1.0 + pre * (1.0 - sigma))
        act_t[lanes, :] = active.T.astype(jnp.bfloat16)

    over_tiles(slopes)
    for other in range(1, n_dp):
        swap_copy(1, other).start()
    act_all[dp] = act_t[pl.ds(pl.multiple_of(dp * pad, 16), pad), :]
    gather_forward(0)

    for c in range(CHUNKS):
        chunk = pl.ds(c * step_rows, step_rows)

        @pl.when(jnp.logical_not(last))
        def _():
            chain_copy(1, c).wait_recv()

        slope = cot_ref[chunk, :].astype(jnp.float32) + returning[chunk, :].astype(jnp.float32)
        slope_all[dp, chunk, :] = slope.astype(jnp.bfloat16)
        if c == CHUNKS - 1:
            gather_start(1)
        acc[chunk, :] = jnp.zeros((step_rows, width), jnp.float32)

        def backward(start, size):
            lanes = pl.ds(start, size)
            back = dot_nt(slope_all[dp, chunk, :], w2[lanes, :])
            pre_slope = back * deriv[chunk, lanes]
            deriv[chunk, lanes] = pre_slope
            acc[chunk, :] += dot_nn(pre_slope.astype(jnp.bfloat16), w1[lanes, :])

        over_tiles(backward)
        norm_slope = acc[chunk, :]
        scale = scale_ref[chunk, 0:1]
        unit = base[chunk, :] * scale
        slope = cot_ref[chunk, :].astype(jnp.float32) + returning[chunk, :].astype(jnp.float32)
        carried = (
            slope
            + scale * (norm_slope - unit * jnp.mean(norm_slope * unit, axis=-1, keepdims=True))
        ).astype(jnp.bfloat16)
        carry_out[chunk, :] = carried
        carry_all[dp, chunk, :] = carried

        @pl.when(jnp.logical_not(first))
        def _():
            chain_copy(1, c).start()

    gather_start(2)

    quarter = term.shape[2]
    per = quarter // depth
    early = code * 2 < n_code

    def term_copy(other):
        target = lax.rem(code + other, n_code)
        return pltpu.make_async_remote_copy(
            src_ref=term.at[target],
            dst_ref=term_in.at[other],
            send_sem=term_send.at[other],
            recv_sem=term_recv.at[other],
            device_id=(dp, target),
            device_id_type=MESH,
        )

    for other in reversed(range(n_code)):
        target = lax.rem(code + other, n_code)
        for piece in range(per):
            start = pl.multiple_of(target * quarter + piece * depth, 16)
            term[target, :, piece * depth : (piece + 1) * depth] = dot_nt(
                carry_all[dp], proj[pl.ds(start, depth), :]
            ).astype(jnp.bfloat16)
        if other:

            @pl.when(early)
            def _():
                term_copy(other).start()

    def turn_over(start, size):
        lanes = pl.ds(start, size)
        pre_t[lanes, :] = deriv[:, lanes].T.astype(jnp.bfloat16)

    over_tiles(turn_over)
    for other in range(1, n_dp):
        swap_copy(2, other).start()
    pre_all[dp] = pre_t[pl.ds(pl.multiple_of(dp * pad, 16), pad), :]

    gather_forward(1)
    gather_forward(2)

    @pl.when(jnp.logical_not(early))
    def _():
        for other in range(1, n_code):
            term_copy(other).start()

    total = term[code].astype(jnp.float32)
    for other in range(1, n_code):
        term_copy(other).wait_recv()
        total += term_in[other].astype(jnp.float32)
    temporal_grad[...] = total.astype(jnp.bfloat16)

    for i in range(3):
        for way in range(2):
            for step in range(chips - 1):
                ring_copy(i, way, step).wait_send()
            for step in range(chips):
                pass_copy(i, way, step).wait_send()
    for c in range(CHUNKS):

        @pl.when(jnp.logical_not(last))
        def _():
            chain_copy(0, c).wait_send()

        @pl.when(jnp.logical_not(first))
        def _():
            chain_copy(1, c).wait_send()

    for i in range(3):
        gather_finish(i)
        for other in range(1, n_dp):
            swap_copy(i, other).wait()
    for other in range(1, n_code):
        term_copy(other).wait_send()


def per_device(
    temporal_out, depth_in, embed, depth_w1, depth_w2, audio_tokens, barge_mask, out_grad
):
    dp_index = lax.axis_index("dp")
    n_code = lax.axis_size("code")
    n_dp = lax.axis_size("dp")
    rows, wide = temporal_out.shape
    depth, width = depth_in.shape[1:]
    share = depth_w1.shape[2]
    pad = -(-share // 16) * 16
    hidden = pad * n_dp
    quarter = wide // n_code
    chips = n_dp // 2
    table = embed[0]
    token_all = audio_tokens[:, 0]
    token_own = lax.dynamic_slice_in_dim(token_all, dp_index * rows, rows, 0)
    embedded = jnp.take(table, token_own, axis=0)
    cotangent = out_grad[:, 0, :] * barge_mask.astype(jnp.bfloat16)[:, None]
    w1_own = jnp.pad(depth_w1[0].T, ((0, pad - share), (0, 0)))
    w2_own = jnp.pad(depth_w2[0].T, ((0, pad - share), (0, 0)))

    bf16, f32 = jnp.bfloat16, jnp.float32
    vmem = pl.BlockSpec(memory_space=pltpu.VMEM)
    hbm = pl.BlockSpec(memory_space=pl.ANY)
    dma = pltpu.SemaphoreType.DMA
    out_shape = (
        jax.ShapeDtypeStruct((rows, quarter), bf16),
        jax.ShapeDtypeStruct((n_dp, rows, depth), bf16),
        jax.ShapeDtypeStruct((n_dp, rows, width), bf16),
        jax.ShapeDtypeStruct((n_dp, rows, width), bf16),
        jax.ShapeDtypeStruct((n_dp, rows, width), bf16),
        jax.ShapeDtypeStruct((n_dp, pad, rows), bf16),
        jax.ShapeDtypeStruct((n_dp, pad, rows), bf16),
    )
    temporal_grad, cols_all, normed_all, slope_all, carry_all, act_all, pre_all = pl.pallas_call(
        functools.partial(chain_kernel, n_dp, n_code),
        out_shape=out_shape,
        in_specs=[vmem, vmem, vmem, hbm, hbm, hbm],
        out_specs=(vmem,) * 7,
        scratch_shapes=[
            pltpu.VMEM((wide, width), bf16),
            pltpu.VMEM((hidden, width), bf16),
            pltpu.VMEM((hidden, width), bf16),
            pltpu.VMEM((rows, width), f32),
            pltpu.VMEM((rows, width), f32),
            pltpu.VMEM((rows, width), bf16),
            pltpu.VMEM((rows, width), bf16),
            pltpu.VMEM((rows, width), bf16),
            pltpu.VMEM((rows, width), bf16),
            pltpu.VMEM((rows, hidden), f32),
            pltpu.VMEM((hidden, rows), bf16),
            pltpu.VMEM((hidden, rows), bf16),
            pltpu.VMEM((rows, 128), f32),
            pltpu.VMEM((n_code, rows, quarter), bf16),
            pltpu.VMEM((n_code, rows, quarter), bf16),
            dma((3, 2, chips)),
            dma((3, 2, chips)),
            dma((3, 2, chips)),
            dma((3, 2, chips)),
            dma((3,)),
            dma((2, CHUNKS)),
            dma((2, CHUNKS)),
            dma((3, 2, chips)),
            dma((3, 2, chips)),
            dma((3, n_dp)),
            dma((3, n_dp)),
            dma((n_code,)),
            dma((n_code,)),
        ],
        compiler_params=pltpu.CompilerParams(
            collective_id=0, has_side_effects=True, vmem_limit_bytes=60 * 1024 * 1024
        ),
        name="depth_chain",
    )(temporal_out, embedded, cotangent, depth_in[0], w1_own, w2_own)

    def over_rows(left, right):
        return lax.dot_general(
            left, right, (((0,), (0,)), ((), ())), preferred_element_type=jnp.float32
        )

    frames = n_dp * rows
    normed = normed_all.reshape(frames, width)
    slope = slope_all.reshape(frames, width)
    carry = carry_all.reshape(frames, width)
    columns = cols_all.reshape(frames, depth)
    pre_rows = pre_all[:, :share, :].transpose(0, 2, 1).reshape(frames, share)
    act_rows = act_all[:, :share, :].transpose(0, 2, 1).reshape(frames, share)
    first_grad = over_rows(normed, pre_rows).astype(bf16)
    second_grad = over_rows(slope, act_rows).astype(bf16)
    proj_grad = over_rows(columns, carry).astype(bf16)
    vocab_local = table.shape[0] // n_dp
    vocab_ids = lax.broadcasted_iota(jnp.int32, (1, vocab_local), 1) + dp_index * vocab_local
    onehot = (token_all[:, None] == vocab_ids).astype(bf16)
    table_grad = over_rows(onehot, carry).astype(bf16)
    return (
        temporal_grad,
        proj_grad[None],
        table_grad[None],
        first_grad[None],
        second_grad[None],
    )


def solution(mesh):
    in_specs = (
        P("dp", None),
        P("code", "dp", None),
        P("code", None, None),
        P("code", None, "dp"),
        P("code", None, "dp"),
        P(None, "code"),
        P("dp"),
        P("dp", "code", None),
    )
    out_specs = (
        P("dp", "code"),
        P("code", "dp", None),
        P("code", "dp", None),
        P("code", None, "dp"),
        P("code", None, "dp"),
    )
    return jax.shard_map(
        per_device, mesh=mesh, in_specs=in_specs, out_specs=out_specs, check_vma=False
    )
```

```python
import functools

import jax
import jax.numpy as jnp
from jax import lax
from jax.experimental import pallas as pl
from jax.experimental.pallas import tpu as pltpu
from jax.sharding import PartitionSpec as P

EPS = 1e-06
MESH = pl.DeviceIdType.MESH
CHUNKS = 2
TILE = 512


def dot_nt(left, right):
    return lax.dot_general(
        left, right, (((1,), (1,)), ((), ())), preferred_element_type=jnp.float32
    )


def dot_nn(left, right):
    return jnp.dot(left, right, preferred_element_type=jnp.float32)


def chain_kernel(
    n_dp,
    n_code,
    temporal,
    embedded,
    cot_ref,
    proj_own,
    w1_own,
    w2_own,
    temporal_grad,
    cols_all,
    normed_all,
    slope_all,
    carry_all,
    act_all,
    pre_all,
    proj,
    w1,
    w2,
    base,
    acc,
    incoming,
    returning,
    state,
    carry_out,
    deriv,
    act_t,
    pre_t,
    scale_ref,
    term,
    term_in,
    ring_send,
    ring_recv,
    pass_send,
    pass_recv,
    own_sem,
    chain_send,
    chain_recv,
    ag_send,
    ag_recv,
    swap_send,
    swap_recv,
    term_send,
    term_recv,
):
    dp = lax.axis_index("dp")
    code = lax.axis_index("code")
    rows, width = base.shape
    hidden = w1.shape[0]
    pad = hidden // n_dp
    depth = proj_own.shape[0]
    half = width // 2
    step_rows = rows // CHUNKS
    chips = n_dp // 2
    core = lax.rem(dp, 2)
    chip = dp // 2
    partner = chip * 2 + 1 - core

    def ring_place(c):
        return jnp.where(lax.rem(c, 2) == 0, c // 2, chips - 1 - c // 2)

    def ring_chip(p):
        p = lax.rem(p + 2 * chips, chips)
        return jnp.where(p < chips // 2, 2 * p, 2 * (chips - 1 - p) + 1)

    place = ring_place(chip)
    right = ring_chip(place + 1) * 2 + core
    left = ring_chip(place - 1) * 2 + core

    barrier = pltpu.get_barrier_semaphore()
    for other in range(1, n_dp):
        pl.semaphore_signal(
            barrier, inc=1, device_id=(lax.rem(dp + other, n_dp), code), device_id_type=MESH
        )
    for other in range(1, n_code):
        pl.semaphore_signal(
            barrier, inc=1, device_id=(dp, lax.rem(code + other, n_code)), device_id_type=MESH
        )
    pl.semaphore_wait(barrier, n_dp + n_code - 2)

    whole = (
        (proj_own, proj, depth),
        (w1_own, w1, pad),
        (w2_own, w2, pad),
    )

    def part(array, size, owner, way):
        start = pl.multiple_of(owner * size, 16)
        return array.at[pl.ds(start, size), pl.ds(way * half, half)]

    def ring_copy(i, way, step):
        own, full, size = whole[i]
        origin = ring_chip(place - step if way == 0 else place + step) * 2 + core
        dst = part(full, size, origin, way)
        src = own.at[:, pl.ds(way * half, half)] if step == 0 else dst
        return pltpu.make_async_remote_copy(
            src_ref=src,
            dst_ref=dst,
            send_sem=ring_send.at[i, way, step],
            recv_sem=ring_recv.at[i, way, step],
            device_id=(right if way == 0 else left, code),
            device_id_type=MESH,
        )

    def pass_copy(i, way, step):
        own, full, size = whole[i]
        origin = ring_chip(place - step if way == 0 else place + step) * 2 + core
        dst = part(full, size, origin, way)
        src = own.at[:, pl.ds(way * half, half)] if step == 0 else dst
        return pltpu.make_async_remote_copy(
            src_ref=src,
            dst_ref=dst,
            send_sem=pass_send.at[i, way, step],
            recv_sem=pass_recv.at[i, way, step],
            device_id=(partner, code),
            device_id_type=MESH,
        )

    def own_copy(i):
        own, full, size = whole[i]
        start = pl.multiple_of(dp * size, 16)
        return pltpu.make_async_copy(own, full.at[pl.ds(start, size), :], own_sem.at[i])

    def add_base(origin, way):
        lanes = pl.ds(way * half, half)
        base[:, lanes] += dot_nn(
            temporal[:, pl.ds(pl.multiple_of(origin * depth, 128), depth)],
            proj[pl.ds(pl.multiple_of(origin * depth, 16), depth), lanes],
        )

    for i in range(3):
        for way in range(2):
            ring_copy(i, way, 0).start()
    for i in range(3):
        for way in range(2):
            pass_copy(i, way, 0).start()
        own_copy(i).start()
    base[...] = embedded[...].astype(jnp.float32)
    own_copy(0).wait()
    for way in range(2):
        add_base(dp, way)
    for step in range(1, chips):
        for i in range(3):
            for way in range(2):
                ring_copy(i, way, step - 1).wait_recv()
                if step < chips - 1:
                    ring_copy(i, way, step).start()
                pass_copy(i, way, step).start()
            if i == 0:
                for way in range(2):
                    add_base(ring_chip(place - step if way == 0 else place + step) * 2 + core, way)
                for way in range(2):
                    pass_copy(0, way, step - 1).wait_recv()
                    add_base(
                        ring_chip(place - step + 1 if way == 0 else place + step - 1) * 2 + 1 - core,
                        way,
                    )
    for way in range(2):
        pass_copy(0, way, chips - 1).wait_recv()
        add_base(
            ring_chip(place - chips + 1 if way == 0 else place + chips - 1) * 2 + 1 - core, way
        )

    def swap_copy(i, other):
        target = lax.rem(dp + other, n_dp)
        if i == 0:
            src = temporal.at[:, pl.ds(pl.multiple_of(target * depth, 128), depth)]
            dst = cols_all.at[dp]
        else:
            table, full = ((act_t, act_all), (pre_t, pre_all))[i - 1]
            src = table.at[pl.ds(pl.multiple_of(target * pad, 16), pad), :]
            dst = full.at[dp]
        return pltpu.make_async_remote_copy(
            src_ref=src,
            dst_ref=dst,
            send_sem=swap_send.at[i, other],
            recv_sem=swap_recv.at[i, other],
            device_id=(target, code),
            device_id_type=MESH,
        )

    gathered = (normed_all, slope_all, carry_all)

    def peer_copy(i, other):
        block = gathered[i].at[dp]
        target = lax.rem(dp + 2 * other, n_dp)
        return pltpu.make_async_remote_copy(
            src_ref=block,
            dst_ref=block,
            send_sem=ag_send.at[i, 0, other],
            recv_sem=ag_recv.at[i, 0, other],
            device_id=(target, code),
            device_id_type=MESH,
        )

    def hand_copy(i, other):
        block = gathered[i].at[lax.rem(dp - 2 * other + n_dp, n_dp)]
        return pltpu.make_async_remote_copy(
            src_ref=block,
            dst_ref=block,
            send_sem=ag_send.at[i, 1, other],
            recv_sem=ag_recv.at[i, 1, other],
            device_id=(partner, code),
            device_id_type=MESH,
        )

    def gather_start(i):
        for other in range(1, chips):
            peer_copy(i, other).start()
        hand_copy(i, 0).start()

    def gather_forward(i):
        for other in range(1, chips):
            peer_copy(i, other).wait_recv()
            hand_copy(i, other).start()

    def gather_finish(i):
        for other in range(1, chips):
            peer_copy(i, other).wait_send()
        for other in range(chips):
            hand_copy(i, other).wait()

    def chain_copy(way, c):
        chunk = pl.ds(c * step_rows, step_rows)
        src, dst = ((state, incoming), (carry_out, returning))[way]
        target = lax.rem(code + (1 if way == 0 else n_code - 1), n_code)
        return pltpu.make_async_remote_copy(
            src_ref=src.at[chunk, :],
            dst_ref=dst.at[chunk, :],
            send_sem=chain_send.at[way, c],
            recv_sem=chain_recv.at[way, c],
            device_id=(dp, target),
            device_id_type=MESH,
        )

    first = code == 0
    last = code == n_code - 1

    @pl.when(first)
    def _():
        incoming[...] = jnp.zeros_like(incoming)

    @pl.when(last)
    def _():
        returning[...] = jnp.zeros_like(returning)

    for i in range(1, 3):
        own_copy(i).wait()
        for way in range(2):
            for step in range(chips):
                pass_copy(i, way, step).wait_recv()
    for other in range(1, n_dp):
        swap_copy(0, other).start()
    cols_all[dp] = temporal[:, pl.ds(pl.multiple_of(dp * depth, 128), depth)]

    tiles = hidden // TILE
    rest = hidden - tiles * TILE

    def over_tiles(body):
        def turn(t, carry):
            body(pl.multiple_of(t * TILE, TILE), TILE)
            return carry

        lax.fori_loop(0, tiles, turn, 0)
        if rest:
            body(tiles * TILE, rest)

    for c in range(CHUNKS):
        chunk = pl.ds(c * step_rows, step_rows)

        @pl.when(jnp.logical_not(first))
        def _():
            chain_copy(0, c).wait_recv()

        resid = base[chunk, :] + incoming[chunk, :].astype(jnp.float32)
        base[chunk, :] = resid
        scale = lax.rsqrt(jnp.mean(resid * resid, axis=-1, keepdims=True) + EPS)
        scale_ref[chunk, :] = jnp.broadcast_to(scale, (step_rows, 128))
        normed_all[dp, chunk, :] = (resid * scale).astype(jnp.bfloat16)
        acc[chunk, :] = resid

        def forward(start, size):
            lanes = pl.ds(start, size)
            pre = dot_nt(normed_all[dp, chunk, :], w1[lanes, :])
            deriv[chunk, lanes] = pre
            active = (pre * jax.nn.sigmoid(pre)).astype(jnp.bfloat16)
            acc[chunk, :] += dot_nn(active, w2[lanes, :])

        over_tiles(forward)
        state[chunk, :] = acc[chunk, :].astype(jnp.bfloat16)

        @pl.when(jnp.logical_not(last))
        def _():
            chain_copy(0, c).start()

    gather_start(0)

    def slopes(start, size):
        lanes = pl.ds(start, size)
        pre = deriv[:, lanes]
        sigma = jax.nn.sigmoid(pre)
        active = pre * sigma
        deriv[:, lanes] = sigma * (1.0 + pre * (1.0 - sigma))
        act_t[lanes, :] = active.T.astype(jnp.bfloat16)

    over_tiles(slopes)
    for other in range(1, n_dp):
        swap_copy(1, other).start()
    act_all[dp] = act_t[pl.ds(pl.multiple_of(dp * pad, 16), pad), :]

    @pl.when(first)
    def _():
        gather_forward(0)


    for c in range(CHUNKS):
        chunk = pl.ds(c * step_rows, step_rows)

        @pl.when(jnp.logical_not(last))
        def _():
            chain_copy(1, c).wait_recv()

        slope = cot_ref[chunk, :].astype(jnp.float32) + returning[chunk, :].astype(jnp.float32)
        slope_all[dp, chunk, :] = slope.astype(jnp.bfloat16)
        if c == CHUNKS - 1:
            gather_start(1)
        acc[chunk, :] = jnp.zeros((step_rows, width), jnp.float32)

        def backward(start, size):
            lanes = pl.ds(start, size)
            back = dot_nt(slope_all[dp, chunk, :], w2[lanes, :])
            pre_slope = back * deriv[chunk, lanes]
            deriv[chunk, lanes] = pre_slope
            acc[chunk, :] += dot_nn(pre_slope.astype(jnp.bfloat16), w1[lanes, :])

        over_tiles(backward)
        norm_slope = acc[chunk, :]
        scale = scale_ref[chunk, 0:1]
        unit = base[chunk, :] * scale
        slope = cot_ref[chunk, :].astype(jnp.float32) + returning[chunk, :].astype(jnp.float32)
        carried = (
            slope
            + scale * (norm_slope - unit * jnp.mean(norm_slope * unit, axis=-1, keepdims=True))
        ).astype(jnp.bfloat16)
        carry_out[chunk, :] = carried
        carry_all[dp, chunk, :] = carried

        @pl.when(jnp.logical_not(first))
        def _():
            chain_copy(1, c).start()

    gather_start(2)

    @pl.when(jnp.logical_not(first))
    def _():
        gather_forward(0)

    quarter = term.shape[2]
    per = quarter // depth
    early = code * 2 < n_code

    def term_copy(other):
        target = lax.rem(code + other, n_code)
        return pltpu.make_async_remote_copy(
            src_ref=term.at[target],
            dst_ref=term_in.at[other],
            send_sem=term_send.at[other],
            recv_sem=term_recv.at[other],
            device_id=(dp, target),
            device_id_type=MESH,
        )

    for other in reversed(range(n_code)):
        target = lax.rem(code + other, n_code)
        for piece in range(per):
            start = pl.multiple_of(target * quarter + piece * depth, 16)
            term[target, :, piece * depth : (piece + 1) * depth] = dot_nt(
                carry_all[dp], proj[pl.ds(start, depth), :]
            ).astype(jnp.bfloat16)
        if other:

            @pl.when(early)
            def _():
                term_copy(other).start()

    def turn_over(start, size):
        lanes = pl.ds(start, size)
        pre_t[lanes, :] = deriv[:, lanes].T.astype(jnp.bfloat16)

    over_tiles(turn_over)
    for other in range(1, n_dp):
        swap_copy(2, other).start()
    pre_all[dp] = pre_t[pl.ds(pl.multiple_of(dp * pad, 16), pad), :]

    gather_forward(1)
    gather_forward(2)

    @pl.when(jnp.logical_not(early))
    def _():
        for other in range(1, n_code):
            term_copy(other).start()

    total = term[code].astype(jnp.float32)
    for other in range(1, n_code):
        term_copy(other).wait_recv()
        total += term_in[other].astype(jnp.float32)
    temporal_grad[...] = total.astype(jnp.bfloat16)

    for i in range(3):
        for way in range(2):
            for step in range(chips - 1):
                ring_copy(i, way, step).wait_send()
            for step in range(chips):
                pass_copy(i, way, step).wait_send()
    for c in range(CHUNKS):

        @pl.when(jnp.logical_not(last))
        def _():
            chain_copy(0, c).wait_send()

        @pl.when(jnp.logical_not(first))
        def _():
            chain_copy(1, c).wait_send()

    for i in range(3):
        gather_finish(i)
        for other in range(1, n_dp):
            swap_copy(i, other).wait()
    for other in range(1, n_code):
        term_copy(other).wait_send()


def per_device(
    temporal_out, depth_in, embed, depth_w1, depth_w2, audio_tokens, barge_mask, out_grad
):
    dp_index = lax.axis_index("dp")
    n_code = lax.axis_size("code")
    n_dp = lax.axis_size("dp")
    rows, wide = temporal_out.shape
    depth, width = depth_in.shape[1:]
    share = depth_w1.shape[2]
    pad = -(-share // 16) * 16
    hidden = pad * n_dp
    quarter = wide // n_code
    chips = n_dp // 2
    table = embed[0]
    token_all = audio_tokens[:, 0]
    token_own = lax.dynamic_slice_in_dim(token_all, dp_index * rows, rows, 0)
    embedded = jnp.take(table, token_own, axis=0)
    cotangent = out_grad[:, 0, :] * barge_mask.astype(jnp.bfloat16)[:, None]
    w1_own = jnp.pad(depth_w1[0].T, ((0, pad - share), (0, 0)))
    w2_own = jnp.pad(depth_w2[0].T, ((0, pad - share), (0, 0)))

    bf16, f32 = jnp.bfloat16, jnp.float32
    vmem = pl.BlockSpec(memory_space=pltpu.VMEM)
    hbm = pl.BlockSpec(memory_space=pl.ANY)
    dma = pltpu.SemaphoreType.DMA
    out_shape = (
        jax.ShapeDtypeStruct((rows, quarter), bf16),
        jax.ShapeDtypeStruct((n_dp, rows, depth), bf16),
        jax.ShapeDtypeStruct((n_dp, rows, width), bf16),
        jax.ShapeDtypeStruct((n_dp, rows, width), bf16),
        jax.ShapeDtypeStruct((n_dp, rows, width), bf16),
        jax.ShapeDtypeStruct((n_dp, pad, rows), bf16),
        jax.ShapeDtypeStruct((n_dp, pad, rows), bf16),
    )
    temporal_grad, cols_all, normed_all, slope_all, carry_all, act_all, pre_all = pl.pallas_call(
        functools.partial(chain_kernel, n_dp, n_code),
        out_shape=out_shape,
        in_specs=[vmem, vmem, vmem, hbm, hbm, hbm],
        out_specs=(vmem,) * 7,
        scratch_shapes=[
            pltpu.VMEM((wide, width), bf16),
            pltpu.VMEM((hidden, width), bf16),
            pltpu.VMEM((hidden, width), bf16),
            pltpu.VMEM((rows, width), f32),
            pltpu.VMEM((rows, width), f32),
            pltpu.VMEM((rows, width), bf16),
            pltpu.VMEM((rows, width), bf16),
            pltpu.VMEM((rows, width), bf16),
            pltpu.VMEM((rows, width), bf16),
            pltpu.VMEM((rows, hidden), f32),
            pltpu.VMEM((hidden, rows), bf16),
            pltpu.VMEM((hidden, rows), bf16),
            pltpu.VMEM((rows, 128), f32),
            pltpu.VMEM((n_code, rows, quarter), bf16),
            pltpu.VMEM((n_code, rows, quarter), bf16),
            dma((3, 2, chips)),
            dma((3, 2, chips)),
            dma((3, 2, chips)),
            dma((3, 2, chips)),
            dma((3,)),
            dma((2, CHUNKS)),
            dma((2, CHUNKS)),
            dma((3, 2, chips)),
            dma((3, 2, chips)),
            dma((3, n_dp)),
            dma((3, n_dp)),
            dma((n_code,)),
            dma((n_code,)),
        ],
        compiler_params=pltpu.CompilerParams(
            collective_id=0, has_side_effects=True, vmem_limit_bytes=60 * 1024 * 1024
        ),
        name="depth_chain",
    )(temporal_out, embedded, cotangent, depth_in[0], w1_own, w2_own)

    def over_rows(left, right):
        return lax.dot_general(
            left, right, (((0,), (0,)), ((), ())), preferred_element_type=jnp.float32
        )

    frames = n_dp * rows
    normed = normed_all.reshape(frames, width)
    slope = slope_all.reshape(frames, width)
    carry = carry_all.reshape(frames, width)
    columns = cols_all.reshape(frames, depth)
    pre_rows = pre_all[:, :share, :].transpose(0, 2, 1).reshape(frames, share)
    act_rows = act_all[:, :share, :].transpose(0, 2, 1).reshape(frames, share)
    first_grad = over_rows(normed, pre_rows).astype(bf16)
    second_grad = over_rows(slope, act_rows).astype(bf16)
    proj_grad = over_rows(columns, carry).astype(bf16)
    vocab_local = table.shape[0] // n_dp
    vocab_ids = lax.broadcasted_iota(jnp.int32, (1, vocab_local), 1) + dp_index * vocab_local
    onehot = (token_all[:, None] == vocab_ids).astype(bf16)
    table_grad = over_rows(onehot, carry).astype(bf16)
    return (
        temporal_grad,
        proj_grad[None],
        table_grad[None],
        first_grad[None],
        second_grad[None],
    )


def solution(mesh):
    in_specs = (
        P("dp", None),
        P("code", "dp", None),
        P("code", None, None),
        P("code", None, "dp"),
        P("code", None, "dp"),
        P(None, "code"),
        P("dp"),
        P("dp", "code", None),
    )
    out_specs = (
        P("dp", "code"),
        P("code", "dp", None),
        P("code", "dp", None),
        P("code", None, "dp"),
        P("code", None, "dp"),
    )
    return jax.shard_map(
        per_device, mesh=mesh, in_specs=in_specs, out_specs=out_specs, check_vma=False
    )
```

```python
import functools

import jax
import jax.numpy as jnp
from jax import lax
from jax.experimental import pallas as pl
from jax.experimental.pallas import tpu as pltpu
from jax.sharding import PartitionSpec as P

EPS = 1e-06
MESH = pl.DeviceIdType.MESH
CHUNKS = 2
TILE = 512


def dot_nt(left, right):
    return lax.dot_general(
        left, right, (((1,), (1,)), ((), ())), preferred_element_type=jnp.float32
    )


def dot_nn(left, right):
    return jnp.dot(left, right, preferred_element_type=jnp.float32)


def chain_kernel(
    n_dp,
    n_code,
    temporal,
    embedded,
    cot_ref,
    proj_own,
    w1_own,
    w2_own,
    temporal_grad,
    cols_all,
    normed_all,
    slope_all,
    carry_all,
    act_all,
    pre_all,
    proj,
    w1,
    w2,
    base,
    acc,
    incoming,
    returning,
    state,
    carry_out,
    deriv,
    act_t,
    pre_t,
    scale_ref,
    term,
    term_in,
    ring_send,
    ring_recv,
    pass_send,
    pass_recv,
    own_sem,
    chain_send,
    chain_recv,
    ag_send,
    ag_recv,
    swap_send,
    swap_recv,
    term_send,
    term_recv,
):
    dp = lax.axis_index("dp")
    code = lax.axis_index("code")
    rows, width = base.shape
    hidden = w1.shape[0]
    pad = hidden // n_dp
    depth = proj_own.shape[0]
    half = width // 2
    step_rows = rows // CHUNKS
    chips = n_dp // 2
    core = lax.rem(dp, 2)
    chip = dp // 2
    partner = chip * 2 + 1 - core

    def ring_place(c):
        return jnp.where(lax.rem(c, 2) == 0, c // 2, chips - 1 - c // 2)

    def ring_chip(p):
        p = lax.rem(p + 2 * chips, chips)
        return jnp.where(p < chips // 2, 2 * p, 2 * (chips - 1 - p) + 1)

    place = ring_place(chip)
    right = ring_chip(place + 1) * 2 + core
    left = ring_chip(place - 1) * 2 + core

    barrier = pltpu.get_barrier_semaphore()
    for other in range(1, n_dp):
        pl.semaphore_signal(
            barrier, inc=1, device_id=(lax.rem(dp + other, n_dp), code), device_id_type=MESH
        )
    for other in range(1, n_code):
        pl.semaphore_signal(
            barrier, inc=1, device_id=(dp, lax.rem(code + other, n_code)), device_id_type=MESH
        )
    pl.semaphore_wait(barrier, n_dp + n_code - 2)

    whole = (
        (proj_own, proj, depth),
        (w1_own, w1, pad),
        (w2_own, w2, pad),
    )

    def part(array, size, owner, way):
        start = pl.multiple_of(owner * size, 16)
        return array.at[pl.ds(start, size), pl.ds(way * half, half)]

    def ring_copy(i, way, step):
        own, full, size = whole[i]
        origin = ring_chip(place - step if way == 0 else place + step) * 2 + core
        dst = part(full, size, origin, way)
        src = own.at[:, pl.ds(way * half, half)] if step == 0 else dst
        return pltpu.make_async_remote_copy(
            src_ref=src,
            dst_ref=dst,
            send_sem=ring_send.at[i, way, step],
            recv_sem=ring_recv.at[i, way, step],
            device_id=(right if way == 0 else left, code),
            device_id_type=MESH,
        )

    def pass_copy(i, way, step):
        own, full, size = whole[i]
        origin = ring_chip(place - step if way == 0 else place + step) * 2 + core
        dst = part(full, size, origin, way)
        src = own.at[:, pl.ds(way * half, half)] if step == 0 else dst
        return pltpu.make_async_remote_copy(
            src_ref=src,
            dst_ref=dst,
            send_sem=pass_send.at[i, way, step],
            recv_sem=pass_recv.at[i, way, step],
            device_id=(partner, code),
            device_id_type=MESH,
        )

    def own_copy(i):
        own, full, size = whole[i]
        start = pl.multiple_of(dp * size, 16)
        return pltpu.make_async_copy(own, full.at[pl.ds(start, size), :], own_sem.at[i])

    def add_base(origin, way):
        lanes = pl.ds(way * half, half)
        base[:, lanes] += dot_nn(
            temporal[:, pl.ds(pl.multiple_of(origin * depth, 128), depth)],
            proj[pl.ds(pl.multiple_of(origin * depth, 16), depth), lanes],
        )

    for i in range(3):
        for way in range(2):
            ring_copy(i, way, 0).start()
    for i in range(3):
        for way in range(2):
            pass_copy(i, way, 0).start()
        own_copy(i).start()
    base[...] = embedded[...].astype(jnp.float32)
    own_copy(0).wait()
    for way in range(2):
        add_base(dp, way)
    for step in range(1, chips):
        for i in range(3):
            for way in range(2):
                ring_copy(i, way, step - 1).wait_recv()
                if step < chips - 1:
                    ring_copy(i, way, step).start()
                pass_copy(i, way, step).start()
            if i == 0:
                for way in range(2):
                    add_base(ring_chip(place - step if way == 0 else place + step) * 2 + core, way)
                for way in range(2):
                    pass_copy(0, way, step - 1).wait_recv()
                    add_base(
                        ring_chip(place - step + 1 if way == 0 else place + step - 1) * 2 + 1 - core,
                        way,
                    )
    for way in range(2):
        pass_copy(0, way, chips - 1).wait_recv()
        add_base(
            ring_chip(place - chips + 1 if way == 0 else place + chips - 1) * 2 + 1 - core, way
        )

    def swap_copy(i, other):
        target = lax.rem(dp + other, n_dp)
        if i == 0:
            src = temporal.at[:, pl.ds(pl.multiple_of(target * depth, 128), depth)]
            dst = cols_all.at[dp]
        else:
            table, full = ((act_t, act_all), (pre_t, pre_all))[i - 1]
            src = table.at[pl.ds(pl.multiple_of(target * pad, 16), pad), :]
            dst = full.at[dp]
        return pltpu.make_async_remote_copy(
            src_ref=src,
            dst_ref=dst,
            send_sem=swap_send.at[i, other],
            recv_sem=swap_recv.at[i, other],
            device_id=(target, code),
            device_id_type=MESH,
        )

    gathered = [(normed_all, 0, rows), (slope_all, 0, rows)] + [
        (carry_all, c * step_rows, step_rows) for c in range(CHUNKS)
    ]

    def gather_block(i, owner):
        full, start, size = gathered[i]
        return full.at[owner, pl.ds(start, size), :]

    def peer_copy(i, other):
        block = gather_block(i, dp)
        target = lax.rem(dp + 2 * other, n_dp)
        return pltpu.make_async_remote_copy(
            src_ref=block,
            dst_ref=block,
            send_sem=ag_send.at[i, 0, other],
            recv_sem=ag_recv.at[i, 0, other],
            device_id=(target, code),
            device_id_type=MESH,
        )

    def hand_copy(i, other):
        block = gather_block(i, lax.rem(dp - 2 * other + n_dp, n_dp))
        return pltpu.make_async_remote_copy(
            src_ref=block,
            dst_ref=block,
            send_sem=ag_send.at[i, 1, other],
            recv_sem=ag_recv.at[i, 1, other],
            device_id=(partner, code),
            device_id_type=MESH,
        )

    def gather_start(i):
        for other in range(1, chips):
            peer_copy(i, other).start()
        hand_copy(i, 0).start()

    def gather_forward(i):
        for other in range(1, chips):
            peer_copy(i, other).wait_recv()
            hand_copy(i, other).start()

    def gather_finish(i):
        for other in range(1, chips):
            peer_copy(i, other).wait_send()
        for other in range(chips):
            hand_copy(i, other).wait()

    def chain_copy(way, c):
        chunk = pl.ds(c * step_rows, step_rows)
        src, dst = ((state, incoming), (carry_out, returning))[way]
        target = lax.rem(code + (1 if way == 0 else n_code - 1), n_code)
        return pltpu.make_async_remote_copy(
            src_ref=src.at[chunk, :],
            dst_ref=dst.at[chunk, :],
            send_sem=chain_send.at[way, c],
            recv_sem=chain_recv.at[way, c],
            device_id=(dp, target),
            device_id_type=MESH,
        )

    first = code == 0
    last = code == n_code - 1

    @pl.when(first)
    def _():
        incoming[...] = jnp.zeros_like(incoming)

    @pl.when(last)
    def _():
        returning[...] = jnp.zeros_like(returning)

    for i in range(1, 3):
        own_copy(i).wait()
        for way in range(2):
            for step in range(chips):
                pass_copy(i, way, step).wait_recv()
    for other in range(1, n_dp):
        swap_copy(0, other).start()
    cols_all[dp] = temporal[:, pl.ds(pl.multiple_of(dp * depth, 128), depth)]

    tiles = hidden // TILE
    rest = hidden - tiles * TILE

    def over_tiles(body):
        def turn(t, carry):
            body(pl.multiple_of(t * TILE, TILE), TILE)
            return carry

        lax.fori_loop(0, tiles, turn, 0)
        if rest:
            body(tiles * TILE, rest)

    for c in range(CHUNKS):
        chunk = pl.ds(c * step_rows, step_rows)

        @pl.when(jnp.logical_not(first))
        def _():
            chain_copy(0, c).wait_recv()

        resid = base[chunk, :] + incoming[chunk, :].astype(jnp.float32)
        base[chunk, :] = resid
        scale = lax.rsqrt(jnp.mean(resid * resid, axis=-1, keepdims=True) + EPS)
        scale_ref[chunk, :] = jnp.broadcast_to(scale, (step_rows, 128))
        normed_all[dp, chunk, :] = (resid * scale).astype(jnp.bfloat16)
        acc[chunk, :] = resid

        def forward(start, size):
            lanes = pl.ds(start, size)
            pre = dot_nt(normed_all[dp, chunk, :], w1[lanes, :])
            deriv[chunk, lanes] = pre
            active = (pre * jax.nn.sigmoid(pre)).astype(jnp.bfloat16)
            acc[chunk, :] += dot_nn(active, w2[lanes, :])

        over_tiles(forward)
        state[chunk, :] = acc[chunk, :].astype(jnp.bfloat16)

        @pl.when(jnp.logical_not(last))
        def _():
            chain_copy(0, c).start()

    gather_start(0)

    def slopes(start, size):
        lanes = pl.ds(start, size)
        pre = deriv[:, lanes]
        sigma = jax.nn.sigmoid(pre)
        active = pre * sigma
        deriv[:, lanes] = sigma * (1.0 + pre * (1.0 - sigma))
        act_t[lanes, :] = active.T.astype(jnp.bfloat16)

    over_tiles(slopes)
    for other in range(1, n_dp):
        swap_copy(1, other).start()
    act_all[dp] = act_t[pl.ds(pl.multiple_of(dp * pad, 16), pad), :]

    @pl.when(first)
    def _():
        gather_forward(0)


    for c in range(CHUNKS):
        chunk = pl.ds(c * step_rows, step_rows)

        @pl.when(jnp.logical_not(last))
        def _():
            chain_copy(1, c).wait_recv()

        slope = cot_ref[chunk, :].astype(jnp.float32) + returning[chunk, :].astype(jnp.float32)
        slope_all[dp, chunk, :] = slope.astype(jnp.bfloat16)
        if c == CHUNKS - 1:
            gather_start(1)
        acc[chunk, :] = jnp.zeros((step_rows, width), jnp.float32)

        def backward(start, size):
            lanes = pl.ds(start, size)
            back = dot_nt(slope_all[dp, chunk, :], w2[lanes, :])
            pre_slope = back * deriv[chunk, lanes]
            deriv[chunk, lanes] = pre_slope
            acc[chunk, :] += dot_nn(pre_slope.astype(jnp.bfloat16), w1[lanes, :])

        over_tiles(backward)
        norm_slope = acc[chunk, :]
        scale = scale_ref[chunk, 0:1]
        unit = base[chunk, :] * scale
        slope = cot_ref[chunk, :].astype(jnp.float32) + returning[chunk, :].astype(jnp.float32)
        carried = (
            slope
            + scale * (norm_slope - unit * jnp.mean(norm_slope * unit, axis=-1, keepdims=True))
        ).astype(jnp.bfloat16)
        carry_out[chunk, :] = carried
        carry_all[dp, chunk, :] = carried

        @pl.when(jnp.logical_not(first))
        def _():
            chain_copy(1, c).start()

        gather_start(2 + c)

    @pl.when(jnp.logical_not(first))
    def _():
        gather_forward(0)

    quarter = term.shape[2]
    per = quarter // depth
    early = code * 2 < n_code

    def term_copy(other):
        target = lax.rem(code + other, n_code)
        return pltpu.make_async_remote_copy(
            src_ref=term.at[target],
            dst_ref=term_in.at[other],
            send_sem=term_send.at[other],
            recv_sem=term_recv.at[other],
            device_id=(dp, target),
            device_id_type=MESH,
        )

    for other in reversed(range(n_code)):
        target = lax.rem(code + other, n_code)
        for piece in range(per):
            start = pl.multiple_of(target * quarter + piece * depth, 16)
            term[target, :, piece * depth : (piece + 1) * depth] = dot_nt(
                carry_all[dp], proj[pl.ds(start, depth), :]
            ).astype(jnp.bfloat16)
        if other:

            @pl.when(early)
            def _():
                term_copy(other).start()

    def turn_over(start, size):
        lanes = pl.ds(start, size)
        pre_t[lanes, :] = deriv[:, lanes].T.astype(jnp.bfloat16)

    over_tiles(turn_over)
    for other in range(1, n_dp):
        swap_copy(2, other).start()
    pre_all[dp] = pre_t[pl.ds(pl.multiple_of(dp * pad, 16), pad), :]

    gather_forward(2)
    gather_forward(1)
    for c in range(1, CHUNKS):
        gather_forward(2 + c)

    @pl.when(jnp.logical_not(early))
    def _():
        for other in range(1, n_code):
            term_copy(other).start()

    total = term[code].astype(jnp.float32)
    for other in range(1, n_code):
        term_copy(other).wait_recv()
        total += term_in[other].astype(jnp.float32)
    temporal_grad[...] = total.astype(jnp.bfloat16)

    for i in range(3):
        for way in range(2):
            for step in range(chips - 1):
                ring_copy(i, way, step).wait_send()
            for step in range(chips):
                pass_copy(i, way, step).wait_send()
    for c in range(CHUNKS):

        @pl.when(jnp.logical_not(last))
        def _():
            chain_copy(0, c).wait_send()

        @pl.when(jnp.logical_not(first))
        def _():
            chain_copy(1, c).wait_send()

    for i in range(len(gathered)):
        gather_finish(i)
    for i in range(3):
        for other in range(1, n_dp):
            swap_copy(i, other).wait()
    for other in range(1, n_code):
        term_copy(other).wait_send()


def per_device(
    temporal_out, depth_in, embed, depth_w1, depth_w2, audio_tokens, barge_mask, out_grad
):
    dp_index = lax.axis_index("dp")
    n_code = lax.axis_size("code")
    n_dp = lax.axis_size("dp")
    rows, wide = temporal_out.shape
    depth, width = depth_in.shape[1:]
    share = depth_w1.shape[2]
    pad = -(-share // 16) * 16
    hidden = pad * n_dp
    quarter = wide // n_code
    chips = n_dp // 2
    table = embed[0]
    token_all = audio_tokens[:, 0]
    token_own = lax.dynamic_slice_in_dim(token_all, dp_index * rows, rows, 0)
    embedded = jnp.take(table, token_own, axis=0)
    cotangent = out_grad[:, 0, :] * barge_mask.astype(jnp.bfloat16)[:, None]
    w1_own = jnp.pad(depth_w1[0].T, ((0, pad - share), (0, 0)))
    w2_own = jnp.pad(depth_w2[0].T, ((0, pad - share), (0, 0)))

    bf16, f32 = jnp.bfloat16, jnp.float32
    vmem = pl.BlockSpec(memory_space=pltpu.VMEM)
    hbm = pl.BlockSpec(memory_space=pl.ANY)
    dma = pltpu.SemaphoreType.DMA
    out_shape = (
        jax.ShapeDtypeStruct((rows, quarter), bf16),
        jax.ShapeDtypeStruct((n_dp, rows, depth), bf16),
        jax.ShapeDtypeStruct((n_dp, rows, width), bf16),
        jax.ShapeDtypeStruct((n_dp, rows, width), bf16),
        jax.ShapeDtypeStruct((n_dp, rows, width), bf16),
        jax.ShapeDtypeStruct((n_dp, pad, rows), bf16),
        jax.ShapeDtypeStruct((n_dp, pad, rows), bf16),
    )
    temporal_grad, cols_all, normed_all, slope_all, carry_all, act_all, pre_all = pl.pallas_call(
        functools.partial(chain_kernel, n_dp, n_code),
        out_shape=out_shape,
        in_specs=[vmem, vmem, vmem, hbm, hbm, hbm],
        out_specs=(vmem,) * 7,
        scratch_shapes=[
            pltpu.VMEM((wide, width), bf16),
            pltpu.VMEM((hidden, width), bf16),
            pltpu.VMEM((hidden, width), bf16),
            pltpu.VMEM((rows, width), f32),
            pltpu.VMEM((rows, width), f32),
            pltpu.VMEM((rows, width), bf16),
            pltpu.VMEM((rows, width), bf16),
            pltpu.VMEM((rows, width), bf16),
            pltpu.VMEM((rows, width), bf16),
            pltpu.VMEM((rows, hidden), f32),
            pltpu.VMEM((hidden, rows), bf16),
            pltpu.VMEM((hidden, rows), bf16),
            pltpu.VMEM((rows, 128), f32),
            pltpu.VMEM((n_code, rows, quarter), bf16),
            pltpu.VMEM((n_code, rows, quarter), bf16),
            dma((3, 2, chips)),
            dma((3, 2, chips)),
            dma((3, 2, chips)),
            dma((3, 2, chips)),
            dma((3,)),
            dma((2, CHUNKS)),
            dma((2, CHUNKS)),
            dma((2 + CHUNKS, 2, chips)),
            dma((2 + CHUNKS, 2, chips)),
            dma((3, n_dp)),
            dma((3, n_dp)),
            dma((n_code,)),
            dma((n_code,)),
        ],
        compiler_params=pltpu.CompilerParams(
            collective_id=0, has_side_effects=True, vmem_limit_bytes=60 * 1024 * 1024
        ),
        name="depth_chain",
    )(temporal_out, embedded, cotangent, depth_in[0], w1_own, w2_own)

    def over_rows(left, right):
        return lax.dot_general(
            left, right, (((0,), (0,)), ((), ())), preferred_element_type=jnp.float32
        )

    frames = n_dp * rows
    normed = normed_all.reshape(frames, width)
    slope = slope_all.reshape(frames, width)
    carry = carry_all.reshape(frames, width)
    columns = cols_all.reshape(frames, depth)
    pre_rows = pre_all[:, :share, :].transpose(0, 2, 1).reshape(frames, share)
    act_rows = act_all[:, :share, :].transpose(0, 2, 1).reshape(frames, share)
    first_grad = over_rows(normed, pre_rows).astype(bf16)
    second_grad = over_rows(slope, act_rows).astype(bf16)
    proj_grad = over_rows(columns, carry).astype(bf16)
    vocab_local = table.shape[0] // n_dp
    vocab_ids = lax.broadcasted_iota(jnp.int32, (1, vocab_local), 1) + dp_index * vocab_local
    onehot = (token_all[:, None] == vocab_ids).astype(bf16)
    table_grad = over_rows(onehot, carry).astype(bf16)
    return (
        temporal_grad,
        proj_grad[None],
        table_grad[None],
        first_grad[None],
        second_grad[None],
    )


def solution(mesh):
    in_specs = (
        P("dp", None),
        P("code", "dp", None),
        P("code", None, None),
        P("code", None, "dp"),
        P("code", None, "dp"),
        P(None, "code"),
        P("dp"),
        P("dp", "code", None),
    )
    out_specs = (
        P("dp", "code"),
        P("code", "dp", None),
        P("code", "dp", None),
        P("code", None, "dp"),
        P("code", None, "dp"),
    )
    return jax.shard_map(
        per_device, mesh=mesh, in_specs=in_specs, out_specs=out_specs, check_vma=False
    )
```
